32 devices in a mesh: dp: 16 (over z, y, x), aug: 2 (over core).
Axes of the slice: x: 2, y: 2, z: 4, core: 2. Of those that a mesh axis runs over, the one named last changes fastest.
Arguments:
- images: bfloat16 [2, 16, 197, 768], P('aug', 'dp'), may hold values from -6 to 6
- out_grads: bfloat16 [2, 16, 197, 768], P('aug', 'dp'), may hold values from -8 to 8
- up_weight_t: bfloat16 [3072, 768], P(('dp', 'aug')), may hold values from -0.21875 to 0.21875
- down_weight_t: bfloat16 [3072, 768], P(('dp', 'aug')), may hold values from -0.21875 to 0.21875
- left_up: bfloat16 [3072, 128], P(('dp', 'aug')), may hold values from -0.109375 to 0.109375
- right_up: bfloat16 [768, 128], replicated, may hold values from -0.21875 to 0.21875
- left_down: bfloat16 [768, 128], replicated, may hold values from -0.21875 to 0.21875
- right_down: bfloat16 [3072, 128], P(('dp', 'aug')), may hold values from -0.109375 to 0.109375
- noise: float32 [2, 128, 128], P(None, 'aug'), may hold values from -6 to 6
Outputs:
- update: float32 [2, 128, 128], P(None, 'aug')
- clip_scales: float32 [16], P('dp')
The draws below stay inside these ranges and needn't reach their ends.
All inputs are finite; a program needn't handle non-finite values.
Results may differ from the reference program's by a relative error of at most 0.0032.
Values may be sent and summed in bfloat16 or wider, within the bound.
A program may use at most 64 MiB of HBM per device.

```python
import math
import jax
import jax.numpy as jnp
from jax import lax

D = 768
FF = 3072
RANK = 128
TOK = 197
IMG_DEV = 1
AUGS = 2
IMAGES = 16


def draw_out_grads(key, part):
    key_scale = jax.random.fold_in(key, 11)
    key_base = jax.random.fold_in(key, 12)
    shape = (AUGS, IMAGES, TOK, D)
    scales = jnp.exp(jax.random.uniform(key_scale, (IMAGES,), jnp.float32, math.log(0.1), 0.0))
    base = jnp.clip(jax.random.normal(key_base, shape, jnp.float32), -7.5, 7.5)
    return (base * scales[None, :, None, None]).astype(jnp.bfloat16)


def steps_of(stream_key, extent, split, low, top_value):
    loudness, own = 1.0, jax.random.fold_in(stream_key, 6)
    for axis_at, shards_of in split:
        heights = jnp.exp(jax.random.uniform(jax.random.fold_in(own, axis_at), (shards_of,), jnp.float32, low / len(split), top_value / len(split)))
        loudness = loudness * jnp.repeat(heights, extent[axis_at] // shards_of).reshape([-1 if axis == axis_at else 1 for axis in range(len(extent))])
    return loudness


def centred(key, extent, spread, reach, pieces=(), held_as=jnp.bfloat16):
    entries = spread * jax.random.normal(key, extent, jnp.float32)
    if pieces:
        entries = entries * steps_of(key, extent, pieces, -0.22, 0.18)
    return jnp.clip(entries, -reach, reach).astype(held_as)


def setup_inputs(seed: int = 0) -> dict:
    splits = jax.random.split(jax.random.key(seed), 10)
    images = centred(splits[0], (AUGS, IMAGES, TOK, D), 1.0, 6.0, ((0, 2), (1, 16)))
    out_grads = draw_out_grads(jax.random.fold_in(splits[9], 71), 0)
    up_weight_t = centred(splits[2], (FF, D), D ** -0.5, 0.21875, ((0, 32),))
    down_weight_t = centred(splits[3], (FF, D), D ** -0.5, 0.21875, ((0, 32),))
    left_up = centred(splits[4], (FF, RANK), FF ** -0.5, 0.109375, ((0, 32),))
    right_up = centred(splits[5], (D, RANK), D ** -0.5, 0.21875)
    left_down = centred(splits[6], (D, RANK), D ** -0.5, 0.21875)
    right_down = centred(splits[7], (FF, RANK), FF ** -0.5, 0.109375, ((0, 32),))
    noise = centred(splits[8], (2, RANK, RANK), 1.0, 6.0, ((1, 2),), jnp.float32)
    return {"images": images, "out_grads": out_grads, "up_weight_t": up_weight_t, "down_weight_t": down_weight_t, "left_up": left_up, "right_up": right_up, "left_down": left_down, "right_down": right_down, "noise": noise}


gelu_coef = 0.7978845608028654
clip_frac = 0.3
noise_mult = 0.05

def gelu_pair(hidden):
    inner = gelu_coef * (hidden + 0.044715 * hidden * hidden * hidden)
    tangent = jnp.tanh(inner)
    value = 0.5 * hidden * (1.0 + tangent)
    slope = 0.5 * (1.0 + tangent) + 0.5 * hidden * (1.0 - tangent * tangent) * gelu_coef * (1.0 + 3.0 * 0.044715 * hidden * hidden)
    return (value, slope)

def contract_last(left, right):
    return lax.dot_general(left, right, (((1,), (1,)), ((), ())), preferred_element_type=jnp.float32)

def block_terms(token_block, grad_block, up_weight_t, down_weight_t, left_up, right_up, left_down, right_down):
    count = token_block.shape[0]
    token_rows = token_block.reshape(-1, token_block.shape[-1])
    grad_rows = grad_block.reshape(-1, grad_block.shape[-1])
    hidden = contract_last(token_rows, up_weight_t)
    activation, slope = gelu_pair(hidden)
    activation = activation.astype(jnp.bfloat16)
    back = contract_last(grad_rows, down_weight_t)
    hidden_grad = (back * slope).astype(jnp.bfloat16)
    v_up = jnp.dot(hidden_grad, left_up, preferred_element_type=jnp.float32).astype(jnp.bfloat16)
    u_up = jnp.dot(token_rows, right_up, preferred_element_type=jnp.float32).astype(jnp.bfloat16)
    u_down = jnp.dot(activation, right_down, preferred_element_type=jnp.float32).astype(jnp.bfloat16)
    v_down = jnp.dot(grad_rows, left_down, preferred_element_type=jnp.float32).astype(jnp.bfloat16)
    shape = (count, TOK, RANK)
    first = jnp.einsum('itr,its->irs', v_up.reshape(shape).astype(jnp.float32), u_up.reshape(shape).astype(jnp.float32))
    second = jnp.einsum('itr,its->irs', v_down.reshape(shape).astype(jnp.float32), u_down.reshape(shape).astype(jnp.float32))
    return jnp.stack([first, second], axis=1)

def reference(images, out_grads, up_weight_t, down_weight_t, left_up, right_up, left_down, right_down, noise):
    blocks = IMAGES // IMG_DEV

    def per_aug(total, pair):
        aug_images, aug_grads = pair
        token_blocks = aug_images.reshape(blocks, IMG_DEV, TOK, D)
        grad_blocks = aug_grads.reshape(blocks, IMG_DEV, TOK, D)

        def one_block(inner):
            return block_terms(inner[0], inner[1], up_weight_t, down_weight_t, left_up, right_up, left_down, right_down)
        terms = lax.map(one_block, (token_blocks, grad_blocks))
        return (total + terms.reshape(IMAGES, 2, RANK, RANK), None)
    start = jnp.zeros((IMAGES, 2, RANK, RANK), jnp.float32)
    total, _ = lax.scan(per_aug, start, (images, out_grads))
    aug_mean = total / AUGS
    squares = lax.optimization_barrier(jnp.sum(aug_mean * aug_mean, axis=(1, 2, 3)))
    norms = jnp.sqrt(squares + 1e-06)
    clip_norm = clip_frac * RANK * math.sqrt(TOK / AUGS)
    clip_scales = jnp.minimum(1.0, clip_norm / norms)
    clipped_sum = lax.optimization_barrier(jnp.sum(clip_scales[:, None, None, None] * aug_mean, axis=0))
    update = (clipped_sum + noise_mult * clip_norm * noise) / jnp.sqrt(jnp.float32(IMAGES))
    return (update, clip_scales)
```

```python
import functools
import math

import jax
import jax.numpy as jnp
from jax import lax
from jax.experimental import pallas as pl
from jax.experimental.pallas import tpu as pltpu
from jax.sharding import PartitionSpec as P

gelu_coef = 0.7978845608028654
clip_frac = 0.3
noise_mult = 0.05
MESH = pl.DeviceIdType.MESH
SIDE = 2
TILE = 32


def gelu_pair(hidden):
    inner = gelu_coef * (hidden + 0.044715 * hidden * hidden * hidden)
    tangent = jnp.tanh(inner)
    value = 0.5 * hidden * (1.0 + tangent)
    slope = 0.5 * (1.0 + tangent) + 0.5 * hidden * (1.0 - tangent * tangent) * gelu_coef * (
        1.0 + 3.0 * 0.044715 * hidden * hidden
    )
    return (value, slope)


def contract_last(left, right):
    return lax.dot_general(
        left, right, (((1,), (1,)), ((), ())), preferred_element_type=jnp.float32
    )


def local(
    images, out_grads, up_weight_t, down_weight_t, left_up, right_up, left_down, right_down, noise
):
    local_augs = images.shape[0]
    local_images = images.shape[1]
    tokens = images.shape[2]
    width = images.shape[3]
    rank = right_up.shape[1]
    token_rows = images.reshape(-1, width)
    grad_rows = out_grads.reshape(-1, width)
    up_piece = lax.all_gather(up_weight_t, ("dp", "aug"), axis=0, tiled=True)
    down_piece = lax.all_gather(down_weight_t, ("dp", "aug"), axis=0, tiled=True)
    left_piece = lax.all_gather(left_up, ("dp", "aug"), axis=0, tiled=True)
    right_piece = lax.all_gather(right_down, ("dp", "aug"), axis=0, tiled=True)
    hidden = contract_last(token_rows, up_piece)
    activation, slope = gelu_pair(hidden)
    back = contract_last(grad_rows, down_piece)
    hidden_grad = (back * slope).astype(jnp.bfloat16)
    first = jnp.dot(hidden_grad, left_piece, preferred_element_type=jnp.float32)
    second = jnp.dot(
        activation.astype(jnp.bfloat16), right_piece, preferred_element_type=jnp.float32
    )
    up_total = first
    down_total = second
    v_up = up_total.astype(jnp.bfloat16)
    u_down = down_total.astype(jnp.bfloat16)
    u_up = jnp.dot(token_rows, right_up, preferred_element_type=jnp.float32).astype(jnp.bfloat16)
    v_down = jnp.dot(grad_rows, left_down, preferred_element_type=jnp.float32).astype(jnp.bfloat16)
    shape = (local_augs, local_images, tokens, rank)
    first = jnp.einsum(
        "aitr,aits->irs",
        v_up.reshape(shape),
        u_up.reshape(shape),
        preferred_element_type=jnp.float32,
    )
    second = jnp.einsum(
        "aitr,aits->irs",
        v_down.reshape(shape),
        u_down.reshape(shape),
        preferred_element_type=jnp.float32,
    )
    local_terms = jnp.stack([first, second], axis=1)
    all_augs = local_augs * lax.axis_size("aug")
    row_sums = lax.psum_scatter(local_terms, "aug", scatter_dimension=2, tiled=True)
    my_rows = row_sums / all_augs
    squares = lax.psum(jnp.sum(my_rows * my_rows, axis=(1, 2, 3)), "aug")
    norms = jnp.sqrt(squares + 1e-06)
    clip_norm = clip_frac * rank * math.sqrt(tokens / all_augs)
    clip_scales = jnp.minimum(1.0, clip_norm / norms)
    clipped_rows = jnp.sum(clip_scales[:, None, None, None] * my_rows, axis=0)
    summed_rows = lax.psum(clipped_rows, "dp")
    all_images = local_images * lax.axis_size("dp")
    update = (summed_rows + noise_mult * clip_norm * noise) / jnp.sqrt(jnp.float32(all_images))
    return (update, clip_scales)


def gather_slot(at, source, length):
    mirror = at // (length // 2)
    at = at + mirror * (length - 1 - 2 * at)
    source = source + mirror * (length - 1 - 2 * source)
    return source + (at - source + length - 1) // length


def slot_source(at, slot, length):
    mirror = at // (length // 2)
    near = at + mirror * (length - 1 - 2 * at)
    source = slot - (near - slot + length) // length
    return source + mirror * (length - 1 - 2 * source)


def kernel(
    line,
    images,
    scale_of,
    x_in,
    g_in,
    up_in,
    down_in,
    left_in,
    right_in,
    right_up_in,
    left_down_in,
    noise_in,
    out,
    clip_out,
    xs,
    gs,
    up,
    down,
    left,
    right,
    right_up,
    left_down,
    noise,
    v_acc,
    u_acc,
    u_up,
    v_down,
    part,
    pieces,
    sums,
    norm_parts,
    line_parts,
    final,
    local_sem,
    tok_send,
    tok_recv,
    w_send,
    w_recv,
    piece_send,
    piece_recv,
    norm_send,
    norm_recv,
    line_send,
    line_recv,
    final_send,
    final_recv,
):
    all_augs, clip_norm = scale_of
    dp = lax.axis_index("dp")
    core = lax.axis_index("aug")
    plane = SIDE * SIDE
    members = plane * 2
    z = dp // plane
    y = (dp // SIDE) % SIDE
    x = dp % SIDE
    rows = up_in.shape[0]
    block = out.shape[1] // plane

    def spot(rel):
        ry, rx, rc = rel // 4, (rel // 2) % 2, rel % 2
        yy = 1 - y if ry else y
        xx = 1 - x if rx else x
        return yy * SIDE + xx, (1 - core if rc else core)

    def member(rel):
        lo, cc = spot(rel)
        return (z * plane + lo, cc)

    def on_line(zz):
        return (zz * plane + y * SIDE + x, core)

    def line_place(rel):
        high, low = z // 2, z % 2
        return on_line((1 - high if rel // 2 else high) * 2 + (1 - low if rel % 2 else low))

    barrier = pltpu.get_barrier_semaphore()
    for rel in range(1, members):
        pl.semaphore_signal(barrier, inc=1, device_id=member(rel), device_id_type=MESH)
    for rel in range(1, line):
        pl.semaphore_signal(barrier, inc=1, device_id=line_place(rel), device_id_type=MESH)

    locals_ = [
        pltpu.make_async_copy(a, b, local_sem.at[n])
        for n, (a, b) in enumerate(
            (
                (x_in, xs.at[0]),
                (g_in, gs.at[0]),
                (right_up_in, right_up),
                (left_down_in, left_down),
                (up_in, up.at[pl.ds(0, rows)]),
                (down_in, down.at[pl.ds(0, rows)]),
                (left_in, left.at[pl.ds(0, rows)]),
                (right_in, right.at[pl.ds(0, rows)]),
                (noise_in, noise),
            )
        )
    ]
    for copy in locals_:
        copy.start()
    pl.semaphore_wait(barrier, members - 1 + line - 1)

    stores = (xs, gs)
    token_sends = []

    def send_token(kind, slot, rel, source=None):
        n = len(token_sends)
        target = stores[kind].at[_xor(slot, rel)]
        copy = pltpu.make_async_remote_copy(
            src_ref=stores[kind].at[slot] if source is None else source,
            dst_ref=target,
            send_sem=tok_send.at[n],
            recv_sem=tok_recv.at[kind, _xor(slot, rel)],
            device_id=member(rel),
            device_id_type=MESH,
        )
        copy.start()
        token_sends.append(copy)

    def await_token(kind, slot):
        pltpu.make_async_copy(
            stores[kind].at[slot], stores[kind].at[slot], tok_recv.at[kind, slot]
        ).wait()

    send_token(0, 0, 2, x_in)
    send_token(1, 0, 4, g_in)

    weight_stores = (up, down, left, right)
    weight_ins = (up_in, down_in, left_in, right_in)

    def weight_copies(source, target, way, slot, from_slot):
        to_row = pl.multiple_of(gather_slot(target, source, line) * rows, TILE)
        return [
            pltpu.make_async_remote_copy(
                src_ref=weight_ins[n] if from_slot == 0 else store.at[pl.ds(from_slot * rows, rows)],
                dst_ref=store.at[pl.ds(to_row, rows)],
                send_sem=w_send.at[way, slot, n],
                recv_sem=w_recv.at[gather_slot(target, source, line), n],
                device_id=on_line(target),
                device_id_type=MESH,
            )
            for n, store in enumerate(weight_stores)
        ]

    def own_weights(act):
        @pl.when(z < line - 1)
        def _():
            for copy in weight_copies(z, z + 1, 0, 0, 0):
                act(copy)

        @pl.when(z > 0)
        def _():
            for copy in weight_copies(z, z - 1, 1, 0, 0):
                act(copy)

    own_weights(lambda copy: copy.start())
    send_token(0, 0, 1, x_in)
    send_token(1, 0, 1, g_in)
    send_token(1, 0, 2, g_in)
    send_token(0, 0, 4, x_in)

    def pass_weights(slot, act):
        source = slot_source(z, slot, line)

        @pl.when(jnp.logical_and(source < z, z < line - 1))
        def _():
            for copy in weight_copies(source, z + 1, 0, slot, slot):
                act(copy)

        @pl.when(jnp.logical_and(source > z, z > 0))
        def _():
            for copy in weight_copies(source, z - 1, 1, slot, slot):
                act(copy)

    def await_weights(slot):
        for n, store in enumerate(weight_stores):
            span = store.at[pl.ds(slot * rows, rows)]
            pltpu.make_async_copy(span, span, w_recv.at[slot, n]).wait()
        pass_weights(slot, lambda copy: copy.start())

    at_end = jnp.logical_or(z == 0, z == line - 1)

    def outer(slot):
        pl.when(at_end)(lambda: await_weights(slot))

    def inner(slot):
        pl.when(jnp.logical_not(at_end))(lambda: await_weights(slot))

    def sides(s):
        u_up[s] = jnp.dot(xs[s], right_up[...], preferred_element_type=jnp.float32).astype(jnp.bfloat16)
        v_down[s] = jnp.dot(gs[s], left_down[...], preferred_element_type=jnp.float32).astype(jnp.bfloat16)

    def cell(s, first_slot, slots, fresh):
        span = pl.ds(first_slot * rows, slots * rows)
        hidden = contract_last(xs[s], up[span, :])
        activation, slope = gelu_pair(hidden)
        back = contract_last(gs[s], down[span, :])
        hidden_grad = (back * slope).astype(jnp.bfloat16)
        v = jnp.dot(hidden_grad, left[span, :], preferred_element_type=jnp.float32)
        u = jnp.dot(activation.astype(jnp.bfloat16), right[span, :], preferred_element_type=jnp.float32)
        if fresh:
            v_acc[s] = v
            u_acc[s] = u
        else:
            v_acc[s] += v
            u_acc[s] += u

    def over(sets, *steps):
        @pl.loop(sets[0], sets[1])
        def _(s):
            for step in steps:
                step(s)

    for copy in locals_:
        copy.wait()
    await_token(0, 1)
    await_token(1, 1)
    over((0, 2), sides)

    await_token(0, 2)
    send_token(0, 2, 4)
    send_token(0, 2, 1)
    await_token(1, 4)
    send_token(1, 4, 2)
    send_token(1, 4, 1)
    await_weights(1)
    inner(2)
    near = functools.partial(cell, first_slot=0, slots=2, fresh=True)
    over((0, 2), near)

    await_token(1, 2)
    send_token(1, 2, 1)
    await_token(0, 4)
    send_token(0, 4, 1)
    await_token(0, 3)
    await_token(1, 3)
    await_token(0, 5)
    await_token(1, 5)
    outer(2)
    inner(3)
    over((2, 6), sides, near)
    await_token(0, 6)
    send_token(0, 6, 1)
    await_token(1, 6)
    send_token(1, 6, 1)
    middle = functools.partial(cell, first_slot=2, slots=1, fresh=False)
    over((0, 6), middle)
    await_token(0, 7)
    await_token(1, 7)
    over((6, 8), sides, near, middle)
    outer(3)

    def contract_first(a, b):
        return lax.dot_general(a, b, (((0,), (0,)), ((), ())), preferred_element_type=jnp.float32)

    piece_copies = []
    for i in range(plane):
        first, second = None, None
        for s in (2 * i, 2 * i + 1):
            cell(s, 3, line - 3, False)
            a = contract_first(v_acc[s].astype(jnp.bfloat16), u_up[s])
            b = contract_first(v_down[s], u_acc[s].astype(jnp.bfloat16))
            first = a if first is None else first + a
            second = b if second is None else second + b
        part[i, 0] = first
        part[i, 1] = second
        for rel in range(1, members):
            lo, cc = spot(rel)
            start = pl.multiple_of((cc * plane + lo) * block, 8)
            copy = pltpu.make_async_remote_copy(
                src_ref=part.at[i, :, pl.ds(start, block), :],
                dst_ref=pieces.at[rel - 1, _xor(i, rel // 2)],
                send_sem=piece_send.at[rel - 1, i],
                recv_sem=piece_recv.at[rel - 1, _xor(i, rel // 2)],
                device_id=member(rel),
                device_id_type=MESH,
            )
            copy.start()
            piece_copies.append(copy)

    my_lo, _ = spot(0)
    mine = pl.ds(pl.multiple_of((core * plane + my_lo) * block, 8), block)
    for i in range(plane):
        total = part[i, :, mine, :]
        for rel in range(1, members):
            span = pieces.at[rel - 1, i]
            pltpu.make_async_copy(span, span, piece_recv.at[rel - 1, i]).wait()
            total = total + pieces[rel - 1, i]
        total = total / all_augs
        sums[i] = total
        squares = jnp.sum(total * total, axis=0)
        norm_parts[0, i] = jnp.sum(squares.reshape(block // 8, 8, squares.shape[1]), axis=0)

    def exchange(buffer, rel, slot, send, recv, place):
        copy = pltpu.make_async_remote_copy(
            src_ref=buffer.at[0],
            dst_ref=buffer.at[slot],
            send_sem=send.at[rel],
            recv_sem=recv.at[rel],
            device_id=place,
            device_id_type=MESH,
        )
        copy.start()
        return copy

    norm_copies = [
        exchange(norm_parts, rel, rel, norm_send, norm_recv, member(rel)) for rel in range(1, members)
    ]
    for copy in norm_copies:
        copy.wait_recv()

    clipped = None
    my_clip = None
    for i in range(plane):
        terms = [norm_parts[rel, _xor(i, rel // 2)] for rel in range(members)]
        while len(terms) > 1:
            terms = [terms[n] + terms[n + 1] for n in range(0, len(terms), 2)]
        square = jnp.sum(terms[0], axis=(0, 1), keepdims=True)
        clip = jnp.minimum(1.0, clip_norm / jnp.sqrt(square + 1e-06))
        if i == 0:
            my_clip = clip
        term = clip[None] * sums[i]
        clipped = term if clipped is None else clipped + term
    line_parts[0] = clipped
    line_copies = [
        exchange(line_parts, rel, rel, line_send, line_recv, line_place(rel)) for rel in range(1, line)
    ]
    clip_out[...] = jnp.broadcast_to(my_clip, clip_out.shape)
    for copy in line_copies:
        copy.wait_recv()
    terms = [line_parts[rel] for rel in range(line)]
    while len(terms) > 1:
        terms = [terms[n] + terms[n + 1] for n in range(0, len(terms), 2)]
    final[my_lo] = terms[0]
    final_copies = []
    for rel in range(2, members, 2):
        copy = pltpu.make_async_remote_copy(
            src_ref=final.at[my_lo],
            dst_ref=final.at[my_lo],
            send_sem=final_send.at[rel // 2],
            recv_sem=final_recv.at[rel // 2],
            device_id=member(rel),
            device_id_type=MESH,
        )
        copy.start()
        final_copies.append(copy)
    for rel in range(2, members, 2):
        lo, _ = spot(rel)
        pltpu.make_async_copy(final.at[lo], final.at[lo], final_recv.at[rel // 2]).wait()
    for q in range(plane):
        rows_q = pl.ds(q * block, block)
        out[:, rows_q, :] = (final[q] + noise_mult * clip_norm * noise[:, rows_q, :]) / math.sqrt(images)

    for copy in token_sends + piece_copies + norm_copies + line_copies + final_copies:
        copy.wait_send()
    own_weights(lambda copy: copy.wait_send())
    for slot in range(1, line):
        pass_weights(slot, lambda copy: copy.wait_send())


def _xor(a, b):
    return a ^ b


def planes(
    line, images, out_grads, up_weight_t, down_weight_t, left_up, right_up, left_down, right_down, noise
):
    tokens, width = images.shape[2:]
    rank = right_up.shape[1]
    rows = up_weight_t.shape[0]
    all_augs = lax.axis_size("aug")
    all_images = lax.axis_size("dp")
    clip_norm = clip_frac * rank * math.sqrt(tokens / all_augs)
    plane = SIDE * SIDE
    members = plane * 2
    block = noise.shape[1] // plane
    lanes = noise.shape[2]
    bf16, f32 = jnp.bfloat16, jnp.float32
    dma = pltpu.SemaphoreType.DMA
    update, clip = pl.pallas_call(
        functools.partial(kernel, line, all_images, (all_augs, clip_norm)),
        out_shape=(
            jax.ShapeDtypeStruct(noise.shape, f32),
            jax.ShapeDtypeStruct((1, 128), f32),
        ),
        in_specs=[pl.BlockSpec(memory_space=pl.ANY)] * 9,
        out_specs=(pl.BlockSpec(memory_space=pltpu.VMEM), pl.BlockSpec(memory_space=pltpu.VMEM)),
        scratch_shapes=[
            pltpu.VMEM((members, tokens, width), bf16),
            pltpu.VMEM((members, tokens, width), bf16),
            pltpu.VMEM((line * rows, width), bf16),
            pltpu.VMEM((line * rows, width), bf16),
            pltpu.VMEM((line * rows, rank), bf16),
            pltpu.VMEM((line * rows, rank), bf16),
            pltpu.VMEM(right_up.shape, bf16),
            pltpu.VMEM(left_down.shape, bf16),
            pltpu.VMEM(noise.shape, f32),
            pltpu.VMEM((members, tokens, rank), f32),
            pltpu.VMEM((members, tokens, rank), f32),
            pltpu.VMEM((members, tokens, rank), bf16),
            pltpu.VMEM((members, tokens, rank), bf16),
            pltpu.VMEM((plane, 2, rank, rank), f32),
            pltpu.VMEM((members - 1, plane, 2, block, lanes), f32),
            pltpu.VMEM((plane, 2, block, lanes), f32),
            pltpu.VMEM((members, plane, 8, lanes), f32),
            pltpu.VMEM((line, 2, block, lanes), f32),
            pltpu.VMEM((plane, 2, block, lanes), f32),
            dma((9,)),
            dma((14,)),
            dma((2, members)),
            dma((2, line, 4)),
            dma((line, 4)),
            dma((members - 1, plane)),
            dma((members - 1, plane)),
            dma((members,)),
            dma((members,)),
            dma((line,)),
            dma((line,)),
            dma((plane,)),
            dma((plane,)),
        ],
        compiler_params=pltpu.CompilerParams(collective_id=0, has_side_effects=True),
        name="planes",
    )(
        images.reshape(tokens, width),
        out_grads.reshape(tokens, width),
        up_weight_t,
        down_weight_t,
        left_up,
        right_down,
        right_up,
        left_down,
        noise,
    )
    return update, clip[0, :1]


def body_of(mesh):
    def body(*args):
        images, up_weight_t, noise = args[0], args[2], args[8]
        plane = SIDE * SIDE
        line = mesh.shape["dp"] // plane
        fits = (
            mesh.shape["aug"] == 2
            and line * plane == mesh.shape["dp"]
            and line == 4
            and images.shape[:2] == (1, 1)
            and up_weight_t.shape[0] % TILE == 0
            and noise.shape[1] % (plane * 8) == 0
        )
        return planes(line, *args) if fits else local(*args)

    return body


def solution(mesh):
    placed = (
        P("aug", "dp", None, None),
        P("aug", "dp", None, None),
        P(("dp", "aug"), None),
        P(("dp", "aug"), None),
        P(("dp", "aug"), None),
        P(),
        P(),
        P(("dp", "aug"), None),
        P(None, "aug", None),
    )
    return jax.shard_map(
        body_of(mesh),
        mesh=mesh,
        in_specs=placed,
        out_specs=(P(None, "aug", None), P("dp")),
        check_vma=False,
    )
```

```python
import functools
import math

import jax
import jax.numpy as jnp
from jax import lax
from jax.experimental import pallas as pl
from jax.experimental.pallas import tpu as pltpu
from jax.sharding import PartitionSpec as P

gelu_coef = 0.7978845608028654
clip_frac = 0.3
noise_mult = 0.05
MESH = pl.DeviceIdType.MESH
SIDE = 2
TILE = 32


def gelu_pair(hidden):
    inner = gelu_coef * (hidden + 0.044715 * hidden * hidden * hidden)
    tangent = jnp.tanh(inner)
    value = 0.5 * hidden * (1.0 + tangent)
    slope = 0.5 * (1.0 + tangent) + 0.5 * hidden * (1.0 - tangent * tangent) * gelu_coef * (
        1.0 + 3.0 * 0.044715 * hidden * hidden
    )
    return (value, slope)


def contract_last(left, right):
    return lax.dot_general(
        left, right, (((1,), (1,)), ((), ())), preferred_element_type=jnp.float32
    )


def local(
    images, out_grads, up_weight_t, down_weight_t, left_up, right_up, left_down, right_down, noise
):
    local_augs = images.shape[0]
    local_images = images.shape[1]
    tokens = images.shape[2]
    width = images.shape[3]
    rank = right_up.shape[1]
    token_rows = images.reshape(-1, width)
    grad_rows = out_grads.reshape(-1, width)
    up_piece = lax.all_gather(up_weight_t, ("dp", "aug"), axis=0, tiled=True)
    down_piece = lax.all_gather(down_weight_t, ("dp", "aug"), axis=0, tiled=True)
    left_piece = lax.all_gather(left_up, ("dp", "aug"), axis=0, tiled=True)
    right_piece = lax.all_gather(right_down, ("dp", "aug"), axis=0, tiled=True)
    hidden = contract_last(token_rows, up_piece)
    activation, slope = gelu_pair(hidden)
    back = contract_last(grad_rows, down_piece)
    hidden_grad = (back * slope).astype(jnp.bfloat16)
    first = jnp.dot(hidden_grad, left_piece, preferred_element_type=jnp.float32)
    second = jnp.dot(
        activation.astype(jnp.bfloat16), right_piece, preferred_element_type=jnp.float32
    )
    up_total = first
    down_total = second
    v_up = up_total.astype(jnp.bfloat16)
    u_down = down_total.astype(jnp.bfloat16)
    u_up = jnp.dot(token_rows, right_up, preferred_element_type=jnp.float32).astype(jnp.bfloat16)
    v_down = jnp.dot(grad_rows, left_down, preferred_element_type=jnp.float32).astype(jnp.bfloat16)
    shape = (local_augs, local_images, tokens, rank)
    first = jnp.einsum(
        "aitr,aits->irs",
        v_up.reshape(shape),
        u_up.reshape(shape),
        preferred_element_type=jnp.float32,
    )
    second = jnp.einsum(
        "aitr,aits->irs",
        v_down.reshape(shape),
        u_down.reshape(shape),
        preferred_element_type=jnp.float32,
    )
    local_terms = jnp.stack([first, second], axis=1)
    all_augs = local_augs * lax.axis_size("aug")
    row_sums = lax.psum_scatter(local_terms, "aug", scatter_dimension=2, tiled=True)
    my_rows = row_sums / all_augs
    squares = lax.psum(jnp.sum(my_rows * my_rows, axis=(1, 2, 3)), "aug")
    norms = jnp.sqrt(squares + 1e-06)
    clip_norm = clip_frac * rank * math.sqrt(tokens / all_augs)
    clip_scales = jnp.minimum(1.0, clip_norm / norms)
    clipped_rows = jnp.sum(clip_scales[:, None, None, None] * my_rows, axis=0)
    summed_rows = lax.psum(clipped_rows, "dp")
    all_images = local_images * lax.axis_size("dp")
    update = (summed_rows + noise_mult * clip_norm * noise) / jnp.sqrt(jnp.float32(all_images))
    return (update, clip_scales)


def gather_slot(at, source, length):
    mirror = at // (length // 2)
    at = at + mirror * (length - 1 - 2 * at)
    source = source + mirror * (length - 1 - 2 * source)
    return source + (at - source + length - 1) // length


def slot_source(at, slot, length):
    mirror = at // (length // 2)
    near = at + mirror * (length - 1 - 2 * at)
    source = slot - (near - slot + length) // length
    return source + mirror * (length - 1 - 2 * source)


def kernel(
    line,
    images,
    scale_of,
    x_in,
    g_in,
    up_in,
    down_in,
    left_in,
    right_in,
    right_up_in,
    left_down_in,
    noise_in,
    out,
    clip_out,
    xs,
    gs,
    up,
    down,
    left,
    right,
    right_up,
    left_down,
    noise,
    v_acc,
    u_acc,
    u_up,
    v_down,
    part,
    sent,
    pieces,
    sums,
    norm_parts,
    line_parts,
    final,
    local_sem,
    tok_send,
    tok_recv,
    w_send,
    w_recv,
    piece_send,
    piece_recv,
    norm_send,
    norm_recv,
    line_send,
    line_recv,
    final_send,
    final_recv,
):
    all_augs, clip_norm = scale_of
    dp = lax.axis_index("dp")
    core = lax.axis_index("aug")
    plane = SIDE * SIDE
    members = plane * 2
    z = dp // plane
    y = (dp // SIDE) % SIDE
    x = dp % SIDE
    rows = up_in.shape[0]
    block = out.shape[1] // plane

    def spot(rel):
        ry, rx, rc = rel // 4, (rel // 2) % 2, rel % 2
        yy = 1 - y if ry else y
        xx = 1 - x if rx else x
        return yy * SIDE + xx, (1 - core if rc else core)

    def member(rel):
        lo, cc = spot(rel)
        return (z * plane + lo, cc)

    def on_line(zz):
        return (zz * plane + y * SIDE + x, core)

    def line_place(rel):
        high, low = z // 2, z % 2
        return on_line((1 - high if rel // 2 else high) * 2 + (1 - low if rel % 2 else low))

    barrier = pltpu.get_barrier_semaphore()
    for rel in (1, 2, 4):
        pl.semaphore_signal(barrier, inc=1, device_id=member(rel), device_id_type=MESH)

    @pl.when(z > 0)
    def _():
        pl.semaphore_signal(barrier, inc=1, device_id=on_line(z - 1), device_id_type=MESH)

    @pl.when(z < line - 1)
    def _():
        pl.semaphore_signal(barrier, inc=1, device_id=on_line(z + 1), device_id_type=MESH)

    at_end = jnp.logical_or(z == 0, z == line - 1)

    locals_ = [
        pltpu.make_async_copy(a, b, local_sem.at[n])
        for n, (a, b) in enumerate(
            (
                (x_in, xs.at[0]),
                (g_in, gs.at[0]),
                (right_up_in, right_up),
                (left_down_in, left_down),
                (up_in, up.at[pl.ds(0, rows)]),
                (down_in, down.at[pl.ds(0, rows)]),
                (left_in, left.at[pl.ds(0, rows)]),
                (right_in, right.at[pl.ds(0, rows)]),
                (noise_in, noise),
            )
        )
    ]
    for copy in locals_:
        copy.start()
    pl.when(at_end)(lambda: pl.semaphore_wait(barrier, 4))
    pl.when(jnp.logical_not(at_end))(lambda: pl.semaphore_wait(barrier, 5))

    stores = (xs, gs)
    token_sends = []

    def send_token(kind, slot, rel, source=None):
        n = len(token_sends)
        target = stores[kind].at[_xor(slot, rel)]
        copy = pltpu.make_async_remote_copy(
            src_ref=stores[kind].at[slot] if source is None else source,
            dst_ref=target,
            send_sem=tok_send.at[n],
            recv_sem=tok_recv.at[kind, _xor(slot, rel)],
            device_id=member(rel),
            device_id_type=MESH,
        )
        copy.start()
        token_sends.append(copy)

    def await_token(kind, slot):
        pltpu.make_async_copy(
            stores[kind].at[slot], stores[kind].at[slot], tok_recv.at[kind, slot]
        ).wait()

    send_token(0, 0, 2, x_in)
    send_token(1, 0, 4, g_in)

    weight_stores = (up, down, left, right)
    weight_ins = (up_in, down_in, left_in, right_in)

    def weight_copies(source, target, way, slot, from_slot):
        to_row = pl.multiple_of(gather_slot(target, source, line) * rows, TILE)
        return [
            pltpu.make_async_remote_copy(
                src_ref=weight_ins[n] if from_slot == 0 else store.at[pl.ds(from_slot * rows, rows)],
                dst_ref=store.at[pl.ds(to_row, rows)],
                send_sem=w_send.at[way, slot, n],
                recv_sem=w_recv.at[gather_slot(target, source, line), n],
                device_id=on_line(target),
                device_id_type=MESH,
            )
            for n, store in enumerate(weight_stores)
        ]

    def own_weights(act):
        @pl.when(z < line - 1)
        def _():
            for copy in weight_copies(z, z + 1, 0, 0, 0):
                act(copy)

        @pl.when(z > 0)
        def _():
            for copy in weight_copies(z, z - 1, 1, 0, 0):
                act(copy)

    own_weights(lambda copy: copy.start())
    send_token(0, 0, 1, x_in)
    send_token(1, 0, 1, g_in)
    send_token(1, 0, 2, g_in)
    send_token(0, 0, 4, x_in)

    def pass_weights(slot, which, act):
        source = slot_source(z, slot, line)

        @pl.when(jnp.logical_and(source < z, z < line - 1))
        def _():
            for n in which:
                act(weight_copies(source, z + 1, 0, slot, slot)[n])

        @pl.when(jnp.logical_and(source > z, z > 0))
        def _():
            for n in which:
                act(weight_copies(source, z - 1, 1, slot, slot)[n])

    every = (0, 1, 2, 3)

    def await_weights(slot, which=every):
        for n in which:
            span = weight_stores[n].at[pl.ds(slot * rows, rows)]
            pltpu.make_async_copy(span, span, w_recv.at[slot, n]).wait()
            pass_weights(slot, (n,), lambda copy: copy.start())

    def outer(slot, which=every):
        pl.when(at_end)(lambda: await_weights(slot, which))

    def inner(slot, which=every):
        pl.when(jnp.logical_not(at_end))(lambda: await_weights(slot, which))

    def sides(s):
        u_up[s] = jnp.dot(xs[s], right_up[...], preferred_element_type=jnp.float32).astype(jnp.bfloat16)
        v_down[s] = jnp.dot(gs[s], left_down[...], preferred_element_type=jnp.float32).astype(jnp.bfloat16)

    def cell(s, first_slot, slots, fresh):
        span = pl.ds(first_slot * rows, slots * rows)
        hidden = contract_last(xs[s], up[span, :])
        activation, slope = gelu_pair(hidden)
        back = contract_last(gs[s], down[span, :])
        hidden_grad = (back * slope).astype(jnp.bfloat16)
        v = jnp.dot(hidden_grad, left[span, :], preferred_element_type=jnp.float32)
        u = jnp.dot(activation.astype(jnp.bfloat16), right[span, :], preferred_element_type=jnp.float32)
        if fresh:
            v_acc[s] = v
            u_acc[s] = u
        else:
            v_acc[s] += v
            u_acc[s] += u

    def over(sets, *steps):
        @pl.loop(sets[0], sets[1])
        def _(s):
            for step in steps:
                step(s)

    for copy in locals_:
        copy.wait()
    await_token(0, 1)
    await_token(1, 1)
    over((0, 2), sides)

    inner(1, (0,))
    inner(2, (0,))
    await_token(0, 2)
    send_token(0, 2, 4)
    send_token(0, 2, 1)
    await_token(1, 4)
    send_token(1, 4, 2)
    send_token(1, 4, 1)
    inner(1, (1, 2, 3))
    inner(2, (1, 2, 3))
    outer(1)
    near = functools.partial(cell, first_slot=0, slots=2, fresh=True)
    over((0, 2), near)
    inner(3, (0,))
    await_token(1, 2)
    send_token(1, 2, 1)
    await_token(0, 4)
    send_token(0, 4, 1)
    await_token(0, 3)
    await_token(1, 3)
    await_token(0, 5)
    await_token(1, 5)
    inner(3, (1, 2, 3))
    over((2, 6), sides, near)
    outer(2)
    await_token(0, 6)
    send_token(0, 6, 1)
    await_token(1, 6)
    send_token(1, 6, 1)
    middle = functools.partial(cell, first_slot=2, slots=1, fresh=False)
    over((0, 6), middle)
    await_token(0, 7)
    await_token(1, 7)
    over((6, 8), sides, near, middle)
    outer(3)

    def contract_first(a, b):
        return lax.dot_general(a, b, (((0,), (0,)), ((), ())), preferred_element_type=jnp.float32)

    piece_copies = []
    for i in range(plane):
        first, second = None, None
        for s in (2 * i, 2 * i + 1):
            cell(s, 3, line - 3, False)
            a = contract_first(v_acc[s].astype(jnp.bfloat16), u_up[s])
            b = contract_first(v_down[s], u_acc[s].astype(jnp.bfloat16))
            first = a if first is None else first + a
            second = b if second is None else second + b
        part[i, 0] = first
        part[i, 1] = second
        sent[i, 0] = first.astype(jnp.bfloat16)
        sent[i, 1] = second.astype(jnp.bfloat16)
        for rel in range(1, members):
            lo, cc = spot(rel)
            start = pl.multiple_of((cc * plane + lo) * block, 16)
            copy = pltpu.make_async_remote_copy(
                src_ref=sent.at[i, :, pl.ds(start, block), :],
                dst_ref=pieces.at[rel - 1, _xor(i, rel // 2)],
                send_sem=piece_send.at[rel - 1, i],
                recv_sem=piece_recv.at[rel - 1, _xor(i, rel // 2)],
                device_id=member(rel),
                device_id_type=MESH,
            )
            copy.start()
            piece_copies.append(copy)

    my_lo, _ = spot(0)
    mine = pl.ds(pl.multiple_of((core * plane + my_lo) * block, 8), block)
    for i in range(plane):
        total = part[i, :, mine, :]
        for rel in range(1, members):
            span = pieces.at[rel - 1, i]
            pltpu.make_async_copy(span, span, piece_recv.at[rel - 1, i]).wait()
            total = total + pieces[rel - 1, i].astype(jnp.float32)
        total = total / all_augs
        sums[i] = total
        squares = jnp.sum(total * total, axis=0)
        norm_parts[0, pl.ds(i, 1), :] = jnp.sum(squares, axis=0, keepdims=True)

    def exchange(buffer, rel, slot, send, recv, place):
        copy = pltpu.make_async_remote_copy(
            src_ref=buffer.at[0],
            dst_ref=buffer.at[slot],
            send_sem=send.at[rel],
            recv_sem=recv.at[rel],
            device_id=place,
            device_id_type=MESH,
        )
        copy.start()
        return copy

    norm_copies = [
        exchange(norm_parts, rel, rel, norm_send, norm_recv, member(rel)) for rel in range(1, members)
    ]
    for copy in norm_copies:
        copy.wait_recv()

    clipped = None
    my_clip = None
    for i in range(plane):
        terms = [norm_parts[rel, pl.ds(_xor(i, rel // 2), 1), :] for rel in range(members)]
        while len(terms) > 1:
            terms = [terms[n] + terms[n + 1] for n in range(0, len(terms), 2)]
        square = jnp.sum(terms[0], axis=(0, 1), keepdims=True)
        clip = jnp.minimum(1.0, clip_norm / jnp.sqrt(square + 1e-06))
        if i == 0:
            my_clip = clip
        term = clip[None] * sums[i]
        clipped = term if clipped is None else clipped + term
    line_parts[0] = clipped
    line_copies = [
        exchange(line_parts, rel, rel, line_send, line_recv, line_place(rel)) for rel in range(1, line)
    ]
    clip_out[...] = jnp.broadcast_to(my_clip, clip_out.shape)
    for copy in line_copies:
        copy.wait_recv()
    terms = [line_parts[rel] for rel in range(line)]
    while len(terms) > 1:
        terms = [terms[n] + terms[n + 1] for n in range(0, len(terms), 2)]
    final[my_lo] = terms[0]
    final_copies = []
    for rel in range(2, members, 2):
        copy = pltpu.make_async_remote_copy(
            src_ref=final.at[my_lo],
            dst_ref=final.at[my_lo],
            send_sem=final_send.at[rel // 2],
            recv_sem=final_recv.at[rel // 2],
            device_id=member(rel),
            device_id_type=MESH,
        )
        copy.start()
        final_copies.append(copy)
    for rel in range(2, members, 2):
        lo, _ = spot(rel)
        pltpu.make_async_copy(final.at[lo], final.at[lo], final_recv.at[rel // 2]).wait()
    for q in range(plane):
        rows_q = pl.ds(q * block, block)
        out[:, rows_q, :] = (final[q] + noise_mult * clip_norm * noise[:, rows_q, :]) / math.sqrt(images)

    for copy in token_sends + piece_copies + norm_copies + line_copies + final_copies:
        copy.wait_send()
    own_weights(lambda copy: copy.wait_send())
    for slot in range(1, line):
        pass_weights(slot, every, lambda copy: copy.wait_send())


def _xor(a, b):
    return a ^ b


def planes(
    line, images, out_grads, up_weight_t, down_weight_t, left_up, right_up, left_down, right_down, noise
):
    tokens, width = images.shape[2:]
    rank = right_up.shape[1]
    rows = up_weight_t.shape[0]
    all_augs = lax.axis_size("aug")
    all_images = lax.axis_size("dp")
    clip_norm = clip_frac * rank * math.sqrt(tokens / all_augs)
    plane = SIDE * SIDE
    members = plane * 2
    block = noise.shape[1] // plane
    lanes = noise.shape[2]
    bf16, f32 = jnp.bfloat16, jnp.float32
    dma = pltpu.SemaphoreType.DMA
    update, clip = pl.pallas_call(
        functools.partial(kernel, line, all_images, (all_augs, clip_norm)),
        out_shape=(
            jax.ShapeDtypeStruct(noise.shape, f32),
            jax.ShapeDtypeStruct((1, 128), f32),
        ),
        in_specs=[pl.BlockSpec(memory_space=pl.ANY)] * 9,
        out_specs=(pl.BlockSpec(memory_space=pltpu.VMEM), pl.BlockSpec(memory_space=pltpu.VMEM)),
        scratch_shapes=[
            pltpu.VMEM((members, tokens, width), bf16),
            pltpu.VMEM((members, tokens, width), bf16),
            pltpu.VMEM((line * rows, width), bf16),
            pltpu.VMEM((line * rows, width), bf16),
            pltpu.VMEM((line * rows, rank), bf16),
            pltpu.VMEM((line * rows, rank), bf16),
            pltpu.VMEM(right_up.shape, bf16),
            pltpu.VMEM(left_down.shape, bf16),
            pltpu.VMEM(noise.shape, f32),
            pltpu.VMEM((members, tokens, rank), f32),
            pltpu.VMEM((members, tokens, rank), f32),
            pltpu.VMEM((members, tokens, rank), bf16),
            pltpu.VMEM((members, tokens, rank), bf16),
            pltpu.VMEM((plane, 2, rank, rank), f32),
            pltpu.VMEM((plane, 2, rank, rank), bf16),
            pltpu.VMEM((members - 1, plane, 2, block, lanes), bf16),
            pltpu.VMEM((plane, 2, block, lanes), f32),
            pltpu.VMEM((members, plane, lanes), f32),
            pltpu.VMEM((line, 2, block, lanes), f32),
            pltpu.VMEM((plane, 2, block, lanes), f32),
            dma((9,)),
            dma((14,)),
            dma((2, members)),
            dma((2, line, 4)),
            dma((line, 4)),
            dma((members - 1, plane)),
            dma((members - 1, plane)),
            dma((members,)),
            dma((members,)),
            dma((line,)),
            dma((line,)),
            dma((plane,)),
            dma((plane,)),
        ],
        compiler_params=pltpu.CompilerParams(collective_id=0, has_side_effects=True),
        name="planes",
    )(
        images.reshape(tokens, width),
        out_grads.reshape(tokens, width),
        up_weight_t,
        down_weight_t,
        left_up,
        right_down,
        right_up,
        left_down,
        noise,
    )
    return update, clip[0, :1]


def body_of(mesh):
    def body(*args):
        images, up_weight_t, noise = args[0], args[2], args[8]
        plane = SIDE * SIDE
        line = mesh.shape["dp"] // plane
        fits = (
            mesh.shape["aug"] == 2
            and line * plane == mesh.shape["dp"]
            and line == 4
            and images.shape[:2] == (1, 1)
            and up_weight_t.shape[0] % TILE == 0
            and noise.shape[1] % (plane * 16) == 0
        )
        return planes(line, *args) if fits else local(*args)

    return body


def solution(mesh):
    placed = (
        P("aug", "dp", None, None),
        P("aug", "dp", None, None),
        P(("dp", "aug"), None),
        P(("dp", "aug"), None),
        P(("dp", "aug"), None),
        P(),
        P(),
        P(("dp", "aug"), None),
        P(None, "aug", None),
    )
    return jax.shard_map(
        body_of(mesh),
        mesh=mesh,
        in_specs=placed,
        out_specs=(P(None, "aug", None), P("dp")),
        check_vma=False,
    )
```

```python
import functools
import math

import jax
import jax.numpy as jnp
from jax import lax
from jax.experimental import pallas as pl
from jax.experimental.pallas import tpu as pltpu
from jax.sharding import PartitionSpec as P

gelu_coef = 0.7978845608028654
clip_frac = 0.3
noise_mult = 0.05
MESH = pl.DeviceIdType.MESH
SIDE = 2
TILE = 32


def gelu_pair(hidden):
    inner = gelu_coef * (hidden + 0.044715 * hidden * hidden * hidden)
    tangent = jnp.tanh(inner)
    value = 0.5 * hidden * (1.0 + tangent)
    slope = 0.5 * (1.0 + tangent) + 0.5 * hidden * (1.0 - tangent * tangent) * gelu_coef * (
        1.0 + 3.0 * 0.044715 * hidden * hidden
    )
    return (value, slope)


def gelu_both(hidden):
    square = hidden * hidden
    tangent = jnp.tanh(hidden * (gelu_coef + gelu_coef * 0.044715 * square))
    half = 0.5 + 0.5 * tangent
    value = hidden * half
    slope = half + value * (1.0 - tangent) * (gelu_coef + 3.0 * 0.044715 * gelu_coef * square)
    return (value, slope)


def contract_last(left, right):
    return lax.dot_general(
        left, right, (((1,), (1,)), ((), ())), preferred_element_type=jnp.float32
    )


def local(
    images, out_grads, up_weight_t, down_weight_t, left_up, right_up, left_down, right_down, noise
):
    local_augs = images.shape[0]
    local_images = images.shape[1]
    tokens = images.shape[2]
    width = images.shape[3]
    rank = right_up.shape[1]
    token_rows = images.reshape(-1, width)
    grad_rows = out_grads.reshape(-1, width)
    up_piece = lax.all_gather(up_weight_t, ("dp", "aug"), axis=0, tiled=True)
    down_piece = lax.all_gather(down_weight_t, ("dp", "aug"), axis=0, tiled=True)
    left_piece = lax.all_gather(left_up, ("dp", "aug"), axis=0, tiled=True)
    right_piece = lax.all_gather(right_down, ("dp", "aug"), axis=0, tiled=True)
    hidden = contract_last(token_rows, up_piece)
    activation, slope = gelu_pair(hidden)
    back = contract_last(grad_rows, down_piece)
    hidden_grad = (back * slope).astype(jnp.bfloat16)
    first = jnp.dot(hidden_grad, left_piece, preferred_element_type=jnp.float32)
    second = jnp.dot(
        activation.astype(jnp.bfloat16), right_piece, preferred_element_type=jnp.float32
    )
    up_total = first
    down_total = second
    v_up = up_total.astype(jnp.bfloat16)
    u_down = down_total.astype(jnp.bfloat16)
    u_up = jnp.dot(token_rows, right_up, preferred_element_type=jnp.float32).astype(jnp.bfloat16)
    v_down = jnp.dot(grad_rows, left_down, preferred_element_type=jnp.float32).astype(jnp.bfloat16)
    shape = (local_augs, local_images, tokens, rank)
    first = jnp.einsum(
        "aitr,aits->irs",
        v_up.reshape(shape),
        u_up.reshape(shape),
        preferred_element_type=jnp.float32,
    )
    second = jnp.einsum(
        "aitr,aits->irs",
        v_down.reshape(shape),
        u_down.reshape(shape),
        preferred_element_type=jnp.float32,
    )
    local_terms = jnp.stack([first, second], axis=1)
    all_augs = local_augs * lax.axis_size("aug")
    row_sums = lax.psum_scatter(local_terms, "aug", scatter_dimension=2, tiled=True)
    my_rows = row_sums / all_augs
    squares = lax.psum(jnp.sum(my_rows * my_rows, axis=(1, 2, 3)), "aug")
    norms = jnp.sqrt(squares + 1e-06)
    clip_norm = clip_frac * rank * math.sqrt(tokens / all_augs)
    clip_scales = jnp.minimum(1.0, clip_norm / norms)
    clipped_rows = jnp.sum(clip_scales[:, None, None, None] * my_rows, axis=0)
    summed_rows = lax.psum(clipped_rows, "dp")
    all_images = local_images * lax.axis_size("dp")
    update = (summed_rows + noise_mult * clip_norm * noise) / jnp.sqrt(jnp.float32(all_images))
    return (update, clip_scales)


def gather_slot(at, source, length):
    mirror = at // (length // 2)
    at = at + mirror * (length - 1 - 2 * at)
    source = source + mirror * (length - 1 - 2 * source)
    return source + (at - source + length - 1) // length


def slot_source(at, slot, length):
    mirror = at // (length // 2)
    near = at + mirror * (length - 1 - 2 * at)
    source = slot - (near - slot + length) // length
    return source + mirror * (length - 1 - 2 * source)


def kernel(
    line,
    images,
    scale_of,
    x_in,
    g_in,
    up_in,
    down_in,
    left_in,
    right_in,
    right_up_in,
    left_down_in,
    noise_in,
    out,
    clip_out,
    xs,
    gs,
    up,
    down,
    left,
    right,
    right_up,
    left_down,
    noise,
    v_acc,
    u_acc,
    u_up,
    v_down,
    part,
    sent,
    pieces,
    sums,
    norm_parts,
    line_parts,
    final,
    up_near,
    up_middle,
    up_far,
    down_near,
    down_middle,
    down_far,
    local_sem,
    tok_send,
    tok_recv,
    w_send,
    w_recv,
    piece_send,
    piece_recv,
    norm_send,
    norm_recv,
    line_send,
    line_recv,
    final_send,
    final_recv,
):
    all_augs, clip_norm = scale_of
    up_t = (up_near, up_middle, up_far)
    down_t = (down_near, down_middle, down_far)
    dp = lax.axis_index("dp")
    core = lax.axis_index("aug")
    plane = SIDE * SIDE
    members = plane * 2
    z = dp // plane
    y = (dp // SIDE) % SIDE
    x = dp % SIDE
    rows = up_in.shape[0]
    tokens = x_in.shape[0]
    held = pl.ds(0, tokens)
    block = out.shape[1] // plane

    def spot(rel):
        ry, rx, rc = rel // 4, (rel // 2) % 2, rel % 2
        yy = 1 - y if ry else y
        xx = 1 - x if rx else x
        return yy * SIDE + xx, (1 - core if rc else core)

    def member(rel):
        lo, cc = spot(rel)
        return (z * plane + lo, cc)

    def on_line(zz):
        return (zz * plane + y * SIDE + x, core)

    def line_place(rel):
        high, low = z // 2, z % 2
        return on_line((1 - high if rel // 2 else high) * 2 + (1 - low if rel % 2 else low))

    barrier = pltpu.get_barrier_semaphore()
    for rel in (1, 2, 4):
        pl.semaphore_signal(barrier, inc=1, device_id=member(rel), device_id_type=MESH)

    @pl.when(z > 0)
    def _():
        pl.semaphore_signal(barrier, inc=1, device_id=on_line(z - 1), device_id_type=MESH)

    @pl.when(z < line - 1)
    def _():
        pl.semaphore_signal(barrier, inc=1, device_id=on_line(z + 1), device_id_type=MESH)

    at_end = jnp.logical_or(z == 0, z == line - 1)

    locals_ = [
        pltpu.make_async_copy(a, b, local_sem.at[n])
        for n, (a, b) in enumerate(
            (
                (x_in, xs.at[0]),
                (g_in, gs.at[0]),
                (right_up_in, right_up),
                (left_down_in, left_down),
                (up_in, up.at[pl.ds(0, rows)]),
                (down_in, down.at[pl.ds(0, rows)]),
                (left_in, left.at[pl.ds(0, rows)]),
                (right_in, right.at[pl.ds(0, rows)]),
                (noise_in, noise),
            )
        )
    ]
    for copy in locals_:
        copy.start()
    pl.when(at_end)(lambda: pl.semaphore_wait(barrier, 4))
    pl.when(jnp.logical_not(at_end))(lambda: pl.semaphore_wait(barrier, 5))

    stores = (xs, gs)
    token_sends = []

    def send_token(kind, slot, rel, source=None):
        n = len(token_sends)
        target = stores[kind].at[_xor(slot, rel)]
        copy = pltpu.make_async_remote_copy(
            src_ref=stores[kind].at[slot] if source is None else source,
            dst_ref=target,
            send_sem=tok_send.at[n],
            recv_sem=tok_recv.at[kind, _xor(slot, rel)],
            device_id=member(rel),
            device_id_type=MESH,
        )
        copy.start()
        token_sends.append(copy)

    def await_token(kind, slot):
        pltpu.make_async_copy(
            stores[kind].at[slot], stores[kind].at[slot], tok_recv.at[kind, slot]
        ).wait()

    send_token(0, 0, 2, x_in)
    send_token(1, 0, 4, g_in)

    weight_stores = (up, down, left, right)
    weight_ins = (up_in, down_in, left_in, right_in)

    def weight_copies(source, target, way, slot, from_slot):
        to_row = pl.multiple_of(gather_slot(target, source, line) * rows, TILE)
        return [
            pltpu.make_async_remote_copy(
                src_ref=weight_ins[n] if from_slot == 0 else store.at[pl.ds(from_slot * rows, rows)],
                dst_ref=store.at[pl.ds(to_row, rows)],
                send_sem=w_send.at[way, slot, n],
                recv_sem=w_recv.at[gather_slot(target, source, line), n],
                device_id=on_line(target),
                device_id_type=MESH,
            )
            for n, store in enumerate(weight_stores)
        ]

    def own_weights(act):
        @pl.when(z < line - 1)
        def _():
            for copy in weight_copies(z, z + 1, 0, 0, 0):
                act(copy)

        @pl.when(z > 0)
        def _():
            for copy in weight_copies(z, z - 1, 1, 0, 0):
                act(copy)

    own_weights(lambda copy: copy.start())
    send_token(0, 0, 1, x_in)
    send_token(1, 0, 1, g_in)
    send_token(1, 0, 2, g_in)
    send_token(0, 0, 4, x_in)

    def pass_weights(slot, which, act):
        source = slot_source(z, slot, line)

        @pl.when(jnp.logical_and(source < z, z < line - 1))
        def _():
            for n in which:
                act(weight_copies(source, z + 1, 0, slot, slot)[n])

        @pl.when(jnp.logical_and(source > z, z > 0))
        def _():
            for n in which:
                act(weight_copies(source, z - 1, 1, slot, slot)[n])

    every = (0, 1, 2, 3)

    def await_weights(slot, which=every):
        for n in which:
            span = weight_stores[n].at[pl.ds(slot * rows, rows)]
            pltpu.make_async_copy(span, span, w_recv.at[slot, n]).wait()
            pass_weights(slot, (n,), lambda copy: copy.start())

    def outer(slot, which=every):
        pl.when(at_end)(lambda: await_weights(slot, which))

    def inner(slot, which=every):
        pl.when(jnp.logical_not(at_end))(lambda: await_weights(slot, which))

    def two(ref, s):
        pad = jnp.zeros((u_up.shape[1] - tokens, ref.shape[2]), ref.dtype)
        return jnp.concatenate([ref[s], pad, ref[s + 1], pad], axis=0)

    def keep(ref, s, value, add=False):
        value = value.reshape(2, ref.shape[1], ref.shape[2])
        ref[pl.ds(s, 2)] = ref[pl.ds(s, 2)] + value if add else value

    def sides(s):
        keep(u_up, s, jnp.dot(two(xs, s), right_up[...], preferred_element_type=jnp.float32).astype(jnp.bfloat16))
        keep(v_down, s, jnp.dot(two(gs, s), left_down[...], preferred_element_type=jnp.float32).astype(jnp.bfloat16))

    groups = {0: 2, 2: 1, 3: line - 3}

    def turn(first_slot):
        span = pl.ds(first_slot * rows, groups[first_slot] * rows)
        n = list(groups).index(first_slot)
        up_t[n][...] = up[span, :].T
        down_t[n][...] = down[span, :].T

    def cell(s, first_slot, fresh):
        slots = groups[first_slot]
        n = list(groups).index(first_slot)
        span = pl.ds(first_slot * rows, slots * rows)
        hidden = jnp.dot(two(xs, s), up_t[n][...], preferred_element_type=jnp.float32)
        activation, slope = gelu_both(hidden)
        back = jnp.dot(two(gs, s), down_t[n][...], preferred_element_type=jnp.float32)
        hidden_grad = (back * slope).astype(jnp.bfloat16)
        v = jnp.dot(hidden_grad, left[span, :], preferred_element_type=jnp.float32)
        u = jnp.dot(activation.astype(jnp.bfloat16), right[span, :], preferred_element_type=jnp.float32)
        keep(v_acc, s, v, not fresh)
        keep(u_acc, s, u, not fresh)

    def over(sets, *steps):
        @pl.loop(sets[0] // 2, sets[1] // 2)
        def _(pair):
            s = pair * 2
            for step in steps:
                step(s)

    for copy in locals_:
        copy.wait()
    await_token(0, 1)
    await_token(1, 1)
    over((0, 2), sides)

    inner(1, (0,))
    inner(2, (0,))
    await_token(0, 2)
    send_token(0, 2, 4)
    send_token(0, 2, 1)
    await_token(1, 4)
    send_token(1, 4, 2)
    send_token(1, 4, 1)
    inner(1, (1, 2, 3))
    inner(2, (1, 2, 3))
    outer(1)
    turn(0)
    near = functools.partial(cell, first_slot=0, fresh=True)
    over((0, 2), near)
    inner(3, (0,))
    await_token(1, 2)
    send_token(1, 2, 1)
    await_token(0, 4)
    send_token(0, 4, 1)
    await_token(0, 3)
    await_token(1, 3)
    await_token(0, 5)
    await_token(1, 5)
    inner(3, (1, 2, 3))
    over((2, 6), sides, near)
    outer(2)
    await_token(0, 6)
    send_token(0, 6, 1)
    await_token(1, 6)
    send_token(1, 6, 1)
    turn(2)
    middle = functools.partial(cell, first_slot=2, fresh=False)
    over((0, 6), middle)
    await_token(0, 7)
    await_token(1, 7)
    over((6, 8), sides, near, middle)
    outer(3)
    turn(3)

    def contract_first(a, b):
        return lax.dot_general(a, b, (((0,), (0,)), ((), ())), preferred_element_type=jnp.float32)

    piece_copies = []
    for i in range(plane):
        first, second = None, None
        cell(2 * i, 3, False)
        for s in (2 * i, 2 * i + 1):
            a = contract_first(v_acc[s, held].astype(jnp.bfloat16), u_up[s, held])
            b = contract_first(v_down[s, held], u_acc[s, held].astype(jnp.bfloat16))
            first = a if first is None else first + a
            second = b if second is None else second + b
        part[i, 0] = first
        part[i, 1] = second
        sent[i, 0] = first.astype(jnp.bfloat16)
        sent[i, 1] = second.astype(jnp.bfloat16)
        for rel in range(1, members):
            lo, cc = spot(rel)
            start = pl.multiple_of((cc * plane + lo) * block, 16)
            copy = pltpu.make_async_remote_copy(
                src_ref=sent.at[i, :, pl.ds(start, block), :],
                dst_ref=pieces.at[rel - 1, _xor(i, rel // 2)],
                send_sem=piece_send.at[rel - 1, i],
                recv_sem=piece_recv.at[rel - 1, _xor(i, rel // 2)],
                device_id=member(rel),
                device_id_type=MESH,
            )
            copy.start()
            piece_copies.append(copy)

    my_lo, _ = spot(0)
    mine = pl.ds(pl.multiple_of((core * plane + my_lo) * block, 8), block)
    for i in range(plane):
        total = part[i, :, mine, :]
        for rel in range(1, members):
            span = pieces.at[rel - 1, i]
            pltpu.make_async_copy(span, span, piece_recv.at[rel - 1, i]).wait()
            total = total + pieces[rel - 1, i].astype(jnp.float32)
        total = total / all_augs
        sums[i] = total
        squares = jnp.sum(total * total, axis=0)
        norm_parts[0, pl.ds(i, 1), :] = jnp.sum(squares, axis=0, keepdims=True)

    def exchange(buffer, rel, slot, send, recv, place):
        copy = pltpu.make_async_remote_copy(
            src_ref=buffer.at[0],
            dst_ref=buffer.at[slot],
            send_sem=send.at[rel],
            recv_sem=recv.at[rel],
            device_id=place,
            device_id_type=MESH,
        )
        copy.start()
        return copy

    norm_copies = [
        exchange(norm_parts, rel, rel, norm_send, norm_recv, member(rel)) for rel in range(1, members)
    ]
    for copy in norm_copies:
        copy.wait_recv()

    clipped = None
    my_clip = None
    for i in range(plane):
        terms = [norm_parts[rel, pl.ds(_xor(i, rel // 2), 1), :] for rel in range(members)]
        while len(terms) > 1:
            terms = [terms[n] + terms[n + 1] for n in range(0, len(terms), 2)]
        square = jnp.sum(terms[0], axis=(0, 1), keepdims=True)
        clip = jnp.minimum(1.0, clip_norm / jnp.sqrt(square + 1e-06))
        if i == 0:
            my_clip = clip
        term = clip[None] * sums[i]
        clipped = term if clipped is None else clipped + term
    line_parts[0] = clipped
    line_copies = [
        exchange(line_parts, rel, rel, line_send, line_recv, line_place(rel)) for rel in range(1, line)
    ]
    clip_out[...] = jnp.broadcast_to(my_clip, clip_out.shape)
    for copy in line_copies:
        copy.wait_recv()
    terms = [line_parts[rel] for rel in range(line)]
    while len(terms) > 1:
        terms = [terms[n] + terms[n + 1] for n in range(0, len(terms), 2)]
    final[my_lo] = terms[0]
    final_copies = []
    for rel in range(2, members, 2):
        copy = pltpu.make_async_remote_copy(
            src_ref=final.at[my_lo],
            dst_ref=final.at[my_lo],
            send_sem=final_send.at[rel // 2],
            recv_sem=final_recv.at[rel // 2],
            device_id=member(rel),
            device_id_type=MESH,
        )
        copy.start()
        final_copies.append(copy)
    for rel in range(2, members, 2):
        lo, _ = spot(rel)
        pltpu.make_async_copy(final.at[lo], final.at[lo], final_recv.at[rel // 2]).wait()
    for q in range(plane):
        rows_q = pl.ds(q * block, block)
        out[:, rows_q, :] = (final[q] + noise_mult * clip_norm * noise[:, rows_q, :]) / math.sqrt(images)

    for copy in token_sends + piece_copies + norm_copies + line_copies + final_copies:
        copy.wait_send()
    own_weights(lambda copy: copy.wait_send())
    for slot in range(1, line):
        pass_weights(slot, every, lambda copy: copy.wait_send())


def _xor(a, b):
    return a ^ b


def planes(
    line, images, out_grads, up_weight_t, down_weight_t, left_up, right_up, left_down, right_down, noise
):
    tokens, width = images.shape[2:]
    rank = right_up.shape[1]
    rows = up_weight_t.shape[0]
    all_augs = lax.axis_size("aug")
    all_images = lax.axis_size("dp")
    clip_norm = clip_frac * rank * math.sqrt(tokens / all_augs)
    plane = SIDE * SIDE
    members = plane * 2
    padded = -(-tokens // 16) * 16
    block = noise.shape[1] // plane
    lanes = noise.shape[2]
    bf16, f32 = jnp.bfloat16, jnp.float32
    dma = pltpu.SemaphoreType.DMA
    update, clip = pl.pallas_call(
        functools.partial(kernel, line, all_images, (all_augs, clip_norm)),
        out_shape=(
            jax.ShapeDtypeStruct(noise.shape, f32),
            jax.ShapeDtypeStruct((1, 128), f32),
        ),
        in_specs=[pl.BlockSpec(memory_space=pl.ANY)] * 9,
        out_specs=(pl.BlockSpec(memory_space=pltpu.VMEM), pl.BlockSpec(memory_space=pltpu.VMEM)),
        scratch_shapes=[
            pltpu.VMEM((members, tokens, width), bf16),
            pltpu.VMEM((members, tokens, width), bf16),
            pltpu.VMEM((line * rows, width), bf16),
            pltpu.VMEM((line * rows, width), bf16),
            pltpu.VMEM((line * rows, rank), bf16),
            pltpu.VMEM((line * rows, rank), bf16),
            pltpu.VMEM(right_up.shape, bf16),
            pltpu.VMEM(left_down.shape, bf16),
            pltpu.VMEM(noise.shape, f32),
            pltpu.VMEM((members, padded, rank), f32),
            pltpu.VMEM((members, padded, rank), f32),
            pltpu.VMEM((members, padded, rank), bf16),
            pltpu.VMEM((members, padded, rank), bf16),
            pltpu.VMEM((plane, 2, rank, rank), f32),
            pltpu.VMEM((plane, 2, rank, rank), bf16),
            pltpu.VMEM((members - 1, plane, 2, block, lanes), bf16),
            pltpu.VMEM((plane, 2, block, lanes), f32),
            pltpu.VMEM((members, plane, lanes), f32),
            pltpu.VMEM((line, 2, block, lanes), f32),
            pltpu.VMEM((plane, 2, block, lanes), f32),
            *[pltpu.VMEM((width, n * rows), bf16) for n in (2, 1, line - 3)] * 2,
            dma((9,)),
            dma((14,)),
            dma((2, members)),
            dma((2, line, 4)),
            dma((line, 4)),
            dma((members - 1, plane)),
            dma((members - 1, plane)),
            dma((members,)),
            dma((members,)),
            dma((line,)),
            dma((line,)),
            dma((plane,)),
            dma((plane,)),
        ],
        compiler_params=pltpu.CompilerParams(collective_id=0, has_side_effects=True),
        name="planes",
    )(
        images.reshape(tokens, width),
        out_grads.reshape(tokens, width),
        up_weight_t,
        down_weight_t,
        left_up,
        right_down,
        right_up,
        left_down,
        noise,
    )
    return update, clip[0, :1]


def body_of(mesh):
    def body(*args):
        images, up_weight_t, noise = args[0], args[2], args[8]
        plane = SIDE * SIDE
        line = mesh.shape["dp"] // plane
        fits = (
            mesh.shape["aug"] == 2
            and line * plane == mesh.shape["dp"]
            and line == 4
            and images.shape[:2] == (1, 1)
            and up_weight_t.shape[0] % TILE == 0
            and noise.shape[1] % (plane * 16) == 0
        )
        return planes(line, *args) if fits else local(*args)

    return body


def solution(mesh):
    placed = (
        P("aug", "dp", None, None),
        P("aug", "dp", None, None),
        P(("dp", "aug"), None),
        P(("dp", "aug"), None),
        P(("dp", "aug"), None),
        P(),
        P(),
        P(("dp", "aug"), None),
        P(None, "aug", None),
    )
    return jax.shard_map(
        body_of(mesh),
        mesh=mesh,
        in_specs=placed,
        out_specs=(P(None, "aug", None), P("dp")),
        check_vma=False,
    )
```
